768 devices in a mesh: blk: 32 (over x, y_lo, core), grp: 24 (over y_hi, z).
Axes of the slice: x: 4, y: 8 (y_hi: 2, y_lo: 4; y = y_hi * 4 + y_lo), z: 12, core: 2. Of those that a mesh axis runs over, the one named last changes fastest.
Arguments:
- query_rows: bfloat16 [393216, 1024], P(('blk', 'grp')), may hold values from -8 to 8
- key_rows: bfloat16 [393216, 1024], P(('blk', 'grp')), may hold values from -8 to 8
- value_rows: bfloat16 [393216, 1024], P(('blk', 'grp')), may hold values from -6 to 6
- tile_lists: int32 [3072, 9], P(('blk', 'grp')), may hold values from -1 to 3071, as said below
- hilbert_order: int32 [393216], P(('blk', 'grp')), may hold values from 0 to 393215, as said below
Outputs:
- attention_out: bfloat16 [393216, 1024], P(('blk', 'grp'))
The draws below stay inside these ranges and needn't reach their ends.
Inputs may be any that keep to these rules, and one draw needn't show every extreme that they name: `tile_lists`: row r lists the key tiles of query tile r. Slot j for j <= 4 holds r - 2 + j or -1; slot 5 + g holds global tile g, the same in every row, the global tiles lying 768 apart. No tile appears twice in a row, and tile r appears in row r. `hilbert_order`: A permutation that maps each aligned block of 512 positions onto itself.
All inputs are finite; a program needn't handle non-finite values.
Results may differ from the reference program's by a relative error of at most 0.0049.
Values may be sent and summed in bfloat16 or wider, within the bound.
A program may use at most 64 MiB of HBM per device.

```python
import jax
import jax.numpy as jnp
from jax import lax

LOCAL_HEADS = 8
HEAD_WIDTH = 128
TILE_POINTS = 128
BAND = 2
NG = 4
TOK_DEV = 512
TOKENS = 393216
N_TILES = 3072
GSTRIDE = 768
SLOT_COUNT = 9


def draw_query_rows(key, part):
    result = jnp.clip(jax.random.normal(jax.random.fold_in(key, 1), (TOKENS, LOCAL_HEADS * HEAD_WIDTH), jnp.float32), -6.0, 6.0)
    return result.astype(jnp.bfloat16)


def draw_key_rows(key, part):
    result = jnp.clip(jax.random.normal(jax.random.fold_in(key, 2), (TOKENS, LOCAL_HEADS * HEAD_WIDTH), jnp.float32), -6.0, 6.0)
    return result.astype(jnp.bfloat16)


def draw_tile_lists(key, part):
    tile_row = jnp.arange(N_TILES, dtype=jnp.int32)[:, None]
    slot_index = jnp.arange(2 * BAND + 1, dtype=jnp.int32)[None, :]
    target = tile_row - BAND + slot_index
    phase = jax.random.randint(jax.random.fold_in(key, 3), (), 0, GSTRIDE).astype(jnp.int32)
    reach = jax.random.randint(jax.random.fold_in(key, 4), (N_TILES, 1), 1, BAND + 1).astype(jnp.int32)
    inside = (target >= 0) & (target < N_TILES)
    near = jnp.abs(slot_index - BAND) <= reach
    not_global = jnp.mod(target - phase, GSTRIDE) != 0
    band_part = jnp.where(inside & near & not_global, target, -1)
    global_part = jnp.broadcast_to(phase + GSTRIDE * jnp.arange(NG, dtype=jnp.int32)[None, :], (N_TILES, NG))
    return jnp.concatenate([band_part, global_part], axis=1).astype(jnp.int32)


def draw_hilbert_order(key, part):
    blocks = TOKENS // TOK_DEV
    ranking = jax.random.randint(jax.random.fold_in(key, 5), (blocks, TOK_DEV), 0, 1 << 16) * TOK_DEV + jnp.arange(TOK_DEV, dtype=jnp.int32)[None, :]
    order = jnp.argsort(ranking, axis=1, stable=True).astype(jnp.int32) + (jnp.arange(blocks, dtype=jnp.int32) * TOK_DEV)[:, None]
    return order.reshape(-1).astype(jnp.int32)


def steps_of(own_key, dims, pieces, least, top_value):
    loudness, own = 1.0, jax.random.fold_in(own_key, 6)
    for axis_at, shards_of in pieces:
        draws = jnp.exp(jax.random.uniform(jax.random.fold_in(own, axis_at), (shards_of,), jnp.float32, least / len(pieces), top_value / len(pieces)))
        loudness = loudness * jnp.repeat(draws, dims[axis_at] // shards_of).reshape([-1 if axis == axis_at else 1 for axis in range(len(dims))])
    return loudness


def noise(stream_key, dims, width, most, cuts=(), kind=jnp.bfloat16):
    values = jax.random.normal(stream_key, dims, jnp.float32) * width
    if len(cuts) > 0:
        values = steps_of(stream_key, dims, cuts, -0.22, 0.18) * values
    return jnp.clip(values, min=-most, max=most).astype(kind)


def setup_inputs(seed: int = 0) -> dict:
    key_of = jax.random.split(jax.random.key(seed), 6)
    return {
        "query_rows": draw_query_rows(jax.random.fold_in(key_of[5], 71), 0),
        "key_rows": draw_key_rows(jax.random.fold_in(key_of[5], 71), 0),
        "value_rows": noise(key_of[2], (TOKENS, LOCAL_HEADS * HEAD_WIDTH), 1.0, 6.0, ((0, 768),)),
        "tile_lists": draw_tile_lists(jax.random.fold_in(key_of[5], 71), 0),
        "hilbert_order": draw_hilbert_order(jax.random.fold_in(key_of[5], 71), 0),
    }


def reference(query_rows, key_rows, value_rows, tile_lists, hilbert_order):
    q_sorted = query_rows[hilbert_order]
    k_sorted = key_rows[hilbert_order]
    v_sorted = value_rows[hilbert_order]
    score_scale = HEAD_WIDTH ** -0.5
    tiled_keys = k_sorted.reshape(N_TILES, TILE_POINTS, LOCAL_HEADS, HEAD_WIDTH)
    tiled_values = v_sorted.reshape(N_TILES, TILE_POINTS, LOCAL_HEADS, HEAD_WIDTH)
    query_tiles = q_sorted.reshape(N_TILES, TILE_POINTS, LOCAL_HEADS, HEAD_WIDTH)

    def one_tile(inputs):
        queries_here, listed = inputs
        selected_tiles = jnp.maximum(listed, 0).astype(jnp.int32)
        selected_keys = tiled_keys[selected_tiles].reshape(SLOT_COUNT * TILE_POINTS, LOCAL_HEADS, HEAD_WIDTH)
        selected_values = tiled_values[selected_tiles].reshape(SLOT_COUNT * TILE_POINTS, LOCAL_HEADS, HEAD_WIDTH)
        allowed = jnp.repeat(listed >= 0, TILE_POINTS)
        scores = jnp.einsum("qhd,khd->hqk", queries_here.astype(jnp.float32), selected_keys.astype(jnp.float32)) * score_scale
        scores = jnp.where(allowed[None, None, :], scores, -1e30)
        row_peak = jnp.max(scores, axis=-1, keepdims=True)
        exponent = jnp.exp(scores - row_peak)
        weights = (exponent / jnp.sum(exponent, axis=-1, keepdims=True)).astype(jnp.bfloat16)
        attended = jnp.einsum("hqk,khd->qhd", weights.astype(jnp.float32), selected_values.astype(jnp.float32))
        return attended.reshape(TILE_POINTS, LOCAL_HEADS * HEAD_WIDTH).astype(jnp.bfloat16)

    attended = lax.map(one_tile, (query_tiles, tile_lists)).reshape(TOKENS, LOCAL_HEADS * HEAD_WIDTH)
    return jnp.zeros_like(attended).at[hilbert_order].set(attended)
```

```python
import functools

import jax
import jax.numpy as jnp
from jax import lax
from jax.experimental import pallas as pl
from jax.experimental.pallas import tpu as pltpu
from jax.sharding import PartitionSpec as P

HEADS = 8
WIDTH = 128
TILE = 128
BAND = 2
NG = 4
ROWS = 512
TILES = ROWS // TILE
HALO = BAND * TILE
GSTRIDE = 768
LOG2E = 1.4426950408889634
SCALE = WIDTH**-0.5 * LOG2E
MASKED = -1e30
NX, NY, NZ, NC = 4, 8, 12, 2
ZL, ZH = 4, 3
YROWS = TILE // NY
ZHEADS = HEADS // ZL
MESH = pl.DeviceIdType.MESH


def place(x, y, z, c):
    return ((x * 4 + y % 4) * NC + c, (y // 4) * NZ + z)


def kernel(
    lists, order_row, k_in, v_in, q_in, out,
    raw, perm, qs, kbuf, vbuf, cand, core_in, half, y_in, chunk, z_in, zsum, zz_in, gbuf,
    peak, mass, acc, att, outv,
    in_sem, out_sem, halo_s, halo_r, core_s, core_r, y_s, y_r, z_s, z_r, zz_s, zz_r,
    za_s, za_r, ya_s, ya_r, xa_s, xa_r, ca_s, ca_r,
):
    blk, grp = lax.axis_index("blk"), lax.axis_index("grp")
    x, yl, c = blk // 8, blk // 2 % 4, blk % 2
    yh, z = grp // NZ, grp % NZ
    y = yh * 4 + yl
    zl, zh = z % ZL, z // ZL
    flat = blk * 24 + grp

    def along(step):
        other = (flat + step + 768) % 768
        return (other // 24, other % 24)

    def remote(src, dst, send, recv, device):
        return pltpu.make_async_remote_copy(
            src_ref=src, dst_ref=dst, send_sem=send, recv_sem=recv, device_id=device, device_id_type=MESH
        )

    loads = [
        pltpu.make_async_copy(src, raw.at[i], in_sem.at[i]) for i, src in enumerate((k_in, v_in, q_in))
    ]
    for load in loads:
        load.start()

    before, after, other_core = along(-1), along(1), place(x, y, z, 1 - c)
    y_to = [place(x, (y + d) % NY, z, c) for d in range(1, NY)]
    z_to = [place(x, y, zh * ZL + (zl + d) % ZL, c) for d in range(1, ZL)]
    zz_to = [place(x, y, (z + ZL * d) % NZ, c) for d in range(1, ZH)]
    x_to = [place((x + d) % NX, y, z, c) for d in range(1, NX)]
    partners = [before, after, other_core, *y_to, *z_to, *zz_to, *x_to]
    barrier = pltpu.get_barrier_semaphore()
    for partner in partners:
        pl.semaphore_signal(barrier, inc=1, device_id=partner, device_id_type=MESH)

    row = lax.rem(order_row[...], ROWS)
    wide = jnp.broadcast_to(row, (TILE, ROWS)).T
    lane = lax.broadcasted_iota(jnp.int32, (ROWS, TILE), 1)
    for b in range(TILES):
        perm[:, b * TILE : (b + 1) * TILE] = jnp.where(wide == lane + b * TILE, 1.0, 0.0).astype(jnp.bfloat16)

    def sort(which, dst, first):
        def pair(i, carry):
            cols = pl.ds(pl.multiple_of(i * 256, 256), 256)
            both = jnp.dot(perm[...], raw[which, :, cols], preferred_element_type=jnp.float32)
            both = both.astype(jnp.bfloat16)
            dst[2 * i, first : first + ROWS, :] = both[:, :WIDTH]
            dst[2 * i + 1, first : first + ROWS, :] = both[:, WIDTH:]
            return carry

        lax.fori_loop(0, HEADS // 2, pair, 0)

    def halo_copies(i, buf):
        return [
            remote(buf.at[:, pl.ds(HALO, HALO)], buf.at[:, pl.ds(HALO + ROWS, HALO)], halo_s.at[2 * i], halo_r.at[2 * i], before),
            remote(buf.at[:, pl.ds(ROWS, HALO)], buf.at[:, pl.ds(0, HALO)], halo_s.at[2 * i + 1], halo_r.at[2 * i + 1], after),
        ]

    loads[0].wait()
    sort(0, kbuf, HALO)
    pl.semaphore_wait(barrier, len(partners))
    halo_k = halo_copies(0, kbuf)
    for copy in halo_k:
        copy.start()
    loads[1].wait()
    sort(1, vbuf, HALO)
    halo_v = halo_copies(1, vbuf)
    for copy in halo_v:
        copy.start()

    spot = lax.rem(lists[0, 2 * BAND + 1], GSTRIDE)
    mine = lax.div(spot, TILES) == flat % (GSTRIDE // TILES)
    parts = [jnp.where(mine & (lax.rem(spot, TILES) == t), 1.0, 0.0).astype(jnp.float32) for t in range(TILES)]

    def candidate(h, carry):
        for i, buf in enumerate((kbuf, vbuf)):
            total = None
            for t in range(TILES):
                term = buf[h, HALO + t * TILE : HALO + (t + 1) * TILE, :].astype(jnp.float32) * parts[t]
                total = term if total is None else total + term
            cand[i, h] = total.astype(jnp.bfloat16)
        return carry

    lax.fori_loop(0, HEADS, candidate, 0)
    core_copy = remote(cand.at[1 - c], core_in, core_s, core_r, other_core)
    core_copy.start()

    loads[2].wait()
    sort(2, qs, 0)

    core_copy.wait_recv()
    half[...] = cand[c] + core_in[...]
    y_copies = []
    for d in range(1, NY):
        rows = pl.ds(pl.multiple_of((y + d) % NY * YROWS, YROWS), YROWS)
        copy = remote(half.at[:, rows], y_in.at[d - 1], y_s.at[d - 1], y_r.at[d - 1], y_to[d - 1])
        copy.start()
        y_copies.append(copy)

    ones = jnp.ones((1, WIDTH), jnp.bfloat16)

    def weigh(q, k, v, biases):
        scores = lax.dot_general(q, k, (((1,), (1,)), ((), ())), preferred_element_type=jnp.float32) * SCALE
        if biases is not None:
            scores = jnp.concatenate(
                [scores[:, i * TILE : (i + 1) * TILE] + bias for i, bias in enumerate(biases)], axis=1
            )
        return scores

    def widened(v):
        return jnp.concatenate([v, jnp.broadcast_to(ones, v.shape)], axis=1)

    def bias_of(t, b):
        return jnp.where(lists[t, b - t + BAND] >= 0, 0.0, MASKED).astype(jnp.float32)

    def local(h, carry):
        for t in range(TILES):
            low, high = max(0, t - BAND), min(TILES, t + BAND + 1)
            keys = slice(HALO + low * TILE, HALO + high * TILE)
            here = slice(t * TILE, (t + 1) * TILE)
            scores = weigh(qs[h, here], kbuf[h, keys], None, [bias_of(t, b) for b in range(low, high)])
            top = jnp.broadcast_to(jnp.max(scores, axis=1, keepdims=True), (TILE, WIDTH))
            weights = jnp.exp2(scores - jnp.tile(top, (1, high - low))).astype(jnp.bfloat16)
            got = jnp.dot(weights, widened(vbuf[h, keys]), preferred_element_type=jnp.float32)
            peak[h, here] = top
            acc[h, here] = got[:, :WIDTH]
            mass[h, here] = got[:, WIDTH:]
        return carry

    def update(h, t, k, v, biases):
        here = slice(t * TILE, (t + 1) * TILE)
        scores = weigh(qs[h, here], k, None, biases)
        old = peak[h, here]
        top = jnp.maximum(old, jnp.broadcast_to(jnp.max(scores, axis=1, keepdims=True), (TILE, WIDTH)))
        weights = jnp.exp2(scores - jnp.tile(top, (1, k.shape[0] // TILE))).astype(jnp.bfloat16)
        got = jnp.dot(weights, widened(v), preferred_element_type=jnp.float32)
        keep = jnp.exp2(old - top)
        return top, acc[h, here] * keep + got[:, :WIDTH], mass[h, here] * keep + got[:, WIDTH:]

    lax.fori_loop(0, 2, local, 0)

    for copy in y_copies:
        copy.wait_recv()
    total = half[:, pl.ds(pl.multiple_of(y * YROWS, YROWS), YROWS)]
    for d in range(1, NY):
        total = total + y_in[d - 1]
    chunk[...] = total
    z_copies = []
    for d in range(1, ZL):
        heads = pl.ds((zl + d) % ZL * ZHEADS, ZHEADS)
        copy = remote(chunk.at[heads], z_in.at[d - 1], z_s.at[d - 1], z_r.at[d - 1], z_to[d - 1])
        copy.start()
        z_copies.append(copy)

    lax.fori_loop(2, 4, local, 0)

    for copy in z_copies:
        copy.wait_recv()
    zsum[...] = chunk[pl.ds(zl * ZHEADS, ZHEADS)] + z_in[0] + z_in[1] + z_in[2]
    zz_copies = []
    for d in range(1, ZH):
        copy = remote(zsum, zz_in.at[d - 1], zz_s.at[d - 1], zz_r.at[d - 1], zz_to[d - 1])
        copy.start()
        zz_copies.append(copy)

    lax.fori_loop(4, 6, local, 0)

    for copy in zz_copies:
        copy.wait_recv()
    own = gbuf.at[c, x, y, pl.ds(zl * ZHEADS, ZHEADS)]
    gbuf[c, x, y, pl.ds(zl * ZHEADS, ZHEADS)] = zsum[...] + zz_in[0] + zz_in[1]
    za_copies = []
    for d in range(1, ZL):
        copy = remote(own, own, za_s.at[d - 1], za_r.at[d - 1], z_to[d - 1])
        copy.start()
        za_copies.append(copy)

    lax.fori_loop(6, 8, local, 0)

    for copy in za_copies:
        copy.wait_recv()
    ya_copies = []
    for d in range(1, NY):
        copy = remote(gbuf.at[c, x, y], gbuf.at[c, x, y], ya_s.at[d - 1], ya_r.at[d - 1], y_to[d - 1])
        copy.start()
        ya_copies.append(copy)
    for copy in ya_copies:
        copy.wait_recv()
    xa_copies = []
    for d in range(1, NX):
        copy = remote(gbuf.at[c, x], gbuf.at[c, x], xa_s.at[d - 1], xa_r.at[d - 1], x_to[d - 1])
        copy.start()
        xa_copies.append(copy)
    ca_copies = []

    def hand_over(i, d):
        tile = gbuf.at[c, (x - d + NX) % NX]
        copy = remote(tile, tile, ca_s.at[i], ca_r.at[i], other_core)
        copy.start()
        ca_copies.append(copy)

    hand_over(0, 0)
    for d in range(1, NX):
        xa_copies[d - 1].wait_recv()
        hand_over(d, d)
    for copy in ca_copies:
        copy.wait_recv()

    def globals_(h, carry):
        k = gbuf[0, :, :, h].reshape(NG * TILE, WIDTH)
        v = gbuf[1, :, :, h].reshape(NG * TILE, WIDTH)
        for t in range(TILES):
            here = slice(t * TILE, (t + 1) * TILE)
            top, sums, share = update(h, t, k, v, None)
            peak[h, here] = top
            acc[h, here] = sums
            mass[h, here] = share
        return carry

    lax.fori_loop(0, HEADS, globals_, 0)

    for copy in halo_k + halo_v:
        copy.wait_recv()

    def edges(h, carry):
        cols = pl.ds(pl.multiple_of(h * WIDTH, WIDTH), WIDTH)
        for t in range(TILES):
            low, high = (t - BAND, 0) if t < BAND else (TILES, t + BAND + 1)
            keys = slice(HALO + low * TILE, HALO + high * TILE)
            biases = [bias_of(t, b) for b in range(low, high)]
            top, sums, share = update(h, t, kbuf[h, keys], vbuf[h, keys], biases)
            att[t * TILE : (t + 1) * TILE, cols] = (sums / share).astype(jnp.bfloat16)
        return carry

    lax.fori_loop(0, HEADS, edges, 0)

    sub = lax.broadcasted_iota(jnp.int32, (ROWS, ROWS), 0)
    perm[...] = jnp.where(jnp.broadcast_to(row, (ROWS, ROWS)) == sub, 1.0, 0.0).astype(jnp.bfloat16)
    stores = []
    for i in range(HEADS // 2):
        cols = slice(i * 256, (i + 1) * 256)
        outv[:, cols] = jnp.dot(perm[...], att[:, cols], preferred_element_type=jnp.float32).astype(jnp.bfloat16)
        store = pltpu.make_async_copy(outv.at[:, cols], out.at[:, cols], out_sem.at[i])
        store.start()
        stores.append(store)
    for copy in halo_k + halo_v + [core_copy] + y_copies + z_copies + zz_copies + za_copies + ya_copies + xa_copies + ca_copies:
        copy.wait_send()
    for store in stores:
        store.wait()


def body(query_rows, key_rows, value_rows, tile_lists, hilbert_order):
    bf16, f32, dma = jnp.bfloat16, jnp.float32, pltpu.SemaphoreType.DMA
    vmem = pltpu.VMEM
    features = HEADS * WIDTH
    padded = ROWS + 2 * HALO
    scratch = [
        vmem((3, ROWS, features), bf16),
        vmem((ROWS, ROWS), bf16),
        vmem((HEADS, ROWS, WIDTH), bf16),
        vmem((HEADS, padded, WIDTH), bf16),
        vmem((HEADS, padded, WIDTH), bf16),
        vmem((2, HEADS, TILE, WIDTH), bf16),
        vmem((HEADS, TILE, WIDTH), bf16),
        vmem((HEADS, TILE, WIDTH), bf16),
        vmem((NY - 1, HEADS, YROWS, WIDTH), bf16),
        vmem((HEADS, YROWS, WIDTH), bf16),
        vmem((ZL - 1, ZHEADS, YROWS, WIDTH), bf16),
        vmem((ZHEADS, YROWS, WIDTH), bf16),
        vmem((ZH - 1, ZHEADS, YROWS, WIDTH), bf16),
        vmem((2, NX, NY, HEADS, YROWS, WIDTH), bf16),
        vmem((HEADS, ROWS, WIDTH), f32),
        vmem((HEADS, ROWS, WIDTH), f32),
        vmem((HEADS, ROWS, WIDTH), f32),
        vmem((ROWS, features), bf16),
        vmem((ROWS, features), bf16),
        dma((3,)),
        dma((HEADS // 2,)),
        dma((4,)),
        dma((4,)),
        dma,
        dma,
    ]
    for count in (NY - 1, ZL - 1, ZH - 1, ZL - 1, NY - 1, NX - 1, NX):
        scratch += [dma((count,)), dma((count,))]
    anywhere = pl.BlockSpec(memory_space=pl.ANY)
    return pl.pallas_call(
        kernel,
        out_shape=jax.ShapeDtypeStruct(query_rows.shape, bf16),
        in_specs=[
            pl.BlockSpec(memory_space=pltpu.SMEM),
            pl.BlockSpec(memory_space=pltpu.VMEM),
            anywhere,
            anywhere,
            anywhere,
        ],
        out_specs=anywhere,
        scratch_shapes=scratch,
        compiler_params=pltpu.CompilerParams(
            collective_id=0, has_side_effects=True, vmem_limit_bytes=60 << 20
        ),
        name="attend",
    )(tile_lists, hilbert_order.reshape(1, ROWS), key_rows, value_rows, query_rows)


def solution(mesh):
    in_specs = (
        P(("blk", "grp"), None),
        P(("blk", "grp"), None),
        P(("blk", "grp"), None),
        P(("blk", "grp"), None),
        P(("blk", "grp")),
    )
    out_specs = P(("blk", "grp"), None)
    return jax.shard_map(body, mesh=mesh, in_specs=in_specs, out_specs=out_specs, check_vma=False)
```

```python
import functools

import jax
import jax.numpy as jnp
from jax import lax
from jax.experimental import pallas as pl
from jax.experimental.pallas import tpu as pltpu
from jax.sharding import PartitionSpec as P

HEADS = 8
WIDTH = 128
TILE = 128
BAND = 2
NG = 4
ROWS = 512
TILES = ROWS // TILE
HALO = BAND * TILE
GSTRIDE = 768
LOG2E = 1.4426950408889634
SCALE = WIDTH**-0.5 * LOG2E
MASKED = -1e30
NX, NY, NZ, NC = 4, 8, 12, 2
YROWS = TILE // NY
GROUP, OWNERS = 6, 4
OWN = HEADS // OWNERS
OWNER_PLANES = tuple(range(GROUP - OWNERS, GROUP + OWNERS))
DIRECT = 4
RELAYS = (9, 10, 2, 1)
NEAR_FIRST = True
MESH = pl.DeviceIdType.MESH


def place(x, y, z, c):
    return ((x * 4 + y % 4) * NC + c, (y // 4) * NZ + z)


def kernel(
    lists, order_row, k_in, v_in, q_in, out,
    raw, perm, picked, qs, kbuf, vbuf, relayed, cand, core_in, half, z_in, zsum, y_in, ysum, zz_in, gbuf,
    peak, mass, acc, att, outv,
    in_sem, out_sem, near_s, halo_r, leg_s, leg_r, relay_s, core_s, core_r, z_s, z_r, y_s, y_r, zz_s, zz_r,
    ya_s, ya_r, za_s, za_r, xa_s, xa_r, ca_s, ca_r,
):
    blk, grp = lax.axis_index("blk"), lax.axis_index("grp")
    x, yl, c = blk // 8, blk // 2 % 4, blk % 2
    yh, z = grp // NZ, grp % NZ
    y = yh * 4 + yl
    flat = blk * 24 + grp
    base = jnp.where(z < GROUP, GROUP - OWNERS, GROUP)
    first, member, own = z // GROUP * GROUP, z % GROUP, z - base
    owner = (own >= 0) & (own < OWNERS)

    def along(step):
        other = (flat + step + 768) % 768
        return (other // 24, other % 24)

    def remote(src, dst, send, recv, device):
        return pltpu.make_async_remote_copy(
            src_ref=src, dst_ref=dst, send_sem=send, recv_sem=recv, device_id=device, device_id_type=MESH
        )

    loads = [
        pltpu.make_async_copy(src, raw.at[i], in_sem.at[i]) for i, src in enumerate((k_in, v_in, q_in))
    ]
    for load in loads:
        load.start()

    other_core = place(x, y, z, 1 - c)
    y_to = [place(x, y + d - jnp.where(y + d >= NY, NY, 0), z, c) for d in range(1, NY)]
    x_to = [place((x + d) % NX, y, z, c) for d in range(1, NX)]
    partner = place(x, y, jnp.where(z < GROUP, z + 4, z - 4), c)
    barrier = pltpu.get_barrier_semaphore()

    def in_group(m):
        return place(x, y, first + m, c)

    def owner_of(k):
        return place(x, y, base + k, c)

    def greet(devices):
        for device in devices:
            pl.semaphore_signal(barrier, inc=1, device_id=device, device_id_type=MESH)

    own_next = [(own + d) % OWNERS for d in range(1, OWNERS)]
    idle = jnp.where(z < GROUP, 0, 10)
    owner_greets = [*y_to, partner, *[owner_of(k) for k in own_next], place(x, y, idle, c), place(x, y, idle + 1, c)]
    other_greets = [owner_of(k) for k in range(OWNERS)]
    after_greets = [along(step) for r in RELAYS for step in (1 + r, r - 11)]
    before_greets = [along(step) for r in RELAYS for step in (r - 12, r)]
    common = [along(-1), along(1), other_core, *x_to]
    greet(common)
    pl.when(owner)(lambda: greet(owner_greets))
    pl.when(jnp.logical_not(owner))(lambda: greet(other_greets))
    pl.when(z == NZ - 1)(lambda: greet(after_greets))
    pl.when(z == 0)(lambda: greet(before_greets))
    for r in RELAYS:
        pl.when(z == r)(functools.partial(greet, [along(step) for step in (-r, 11 - r, -r - 1, 12 - r)]))

    def greeted():
        for plane in range(NZ):
            count = len(common)
            count += len(owner_greets) if plane in OWNER_PLANES else len(other_greets)
            count += 2 * len(RELAYS) if plane in (0, NZ - 1) else 0
            count += 4 if plane in RELAYS else 0
            pl.when(z == plane)(functools.partial(pl.semaphore_wait, barrier, count))

    row = lax.rem(order_row[...], ROWS)
    wide = jnp.broadcast_to(row, (TILE, ROWS)).T
    lane = lax.broadcasted_iota(jnp.int32, (ROWS, TILE), 1)
    for b in range(TILES):
        perm[:, b * TILE : (b + 1) * TILE] = jnp.where(wide == lane + b * TILE, 1.0, 0.0).astype(jnp.bfloat16)

    def sort(which, dst, start):
        def pair(i, carry):
            cols = pl.ds(pl.multiple_of(i * 256, 256), 256)
            both = jnp.dot(perm[...], raw[which, :, cols], preferred_element_type=jnp.float32)
            both = both.astype(jnp.bfloat16)
            dst[2 * i, start : start + ROWS, :] = both[:, :WIDTH]
            dst[2 * i + 1, start : start + ROWS, :] = both[:, WIDTH:]
            return carry

        lax.fori_loop(0, HEADS // 2, pair, 0)

    bufs = (kbuf, vbuf)
    send_rows = (pl.ds(ROWS, HALO), pl.ds(HALO, HALO))
    land_rows = (pl.ds(0, HALO), pl.ds(HALO + ROWS, HALO))

    def straight(i, way, heads):
        here = pl.ds(0, heads)
        return remote(
            bufs[i].at[here, send_rows[way]], bufs[i].at[here, land_rows[way]],
            near_s.at[i, way], halo_r.at[i, way, 0], along(1 - 2 * way),
        )

    def to_relay(i, way, p):
        return remote(
            bufs[i].at[DIRECT + p, send_rows[way]], relayed.at[i, way],
            leg_s.at[i, p], leg_r.at[i, way], along(RELAYS[p] + (1, -12)[way]),
        )

    def from_relay(i, way, p):
        return remote(
            relayed.at[i, way], bufs[i].at[DIRECT + p, land_rows[way]],
            relay_s.at[i, way], halo_r.at[i, way, p + 1], along((0, 11)[way] - RELAYS[p]),
        )

    edges = ((NZ - 1, 0), (0, 1))
    seam_in = (0, NZ - 1)

    def send_far(i):
        for plane, way in edges:
            @pl.when(z == plane)
            def _():
                for p in range(len(RELAYS)):
                    to_relay(i, way, p).start()
                straight(i, way, DIRECT).start()

    def send_near(i):
        for plane, way in edges:
            pl.when(z != plane)(lambda: straight(i, way, HEADS).start())

    def forward(i):
        for p, r in enumerate(RELAYS):
            @pl.when(z == r)
            def _():
                for way in (0, 1) if r >= GROUP else (1, 0):
                    to_relay(i, way, p).wait_recv()
                    from_relay(i, way, p).start()

    def halo_sent():
        for i in range(2):
            for plane, way in edges:
                @pl.when(z == plane)
                def _():
                    for p in range(len(RELAYS)):
                        to_relay(i, way, p).wait_send()
                    straight(i, way, DIRECT).wait_send()

                pl.when(z != plane)(lambda: straight(i, way, HEADS).wait_send())
            for p, r in enumerate(RELAYS):
                @pl.when(z == r)
                def _():
                    for way in range(2):
                        from_relay(i, way, p).wait_send()

    def halo_landed(way, far):
        @pl.when((z == seam_in[way]) == far)
        def _():
            for i in range(2):
                if far:
                    straight(i, way, DIRECT).wait_recv()
                    for p in range(len(RELAYS)):
                        from_relay(i, way, p).wait_recv()
                else:
                    straight(i, way, HEADS).wait_recv()

    spot = lax.rem(lists[0, 2 * BAND + 1], GSTRIDE)
    mine = lax.div(spot, TILES) == flat % (GSTRIDE // TILES)
    parts = [jnp.where(mine & (lax.rem(spot, TILES) == t), 1.0, 0.0).astype(jnp.bfloat16) for t in range(TILES)]
    pick = None
    for t in range(TILES):
        term = perm[t * TILE : (t + 1) * TILE, :] * parts[t]
        pick = term if pick is None else pick + term
    picked[...] = pick

    def candidate(i):
        def pair(j, carry):
            cols = pl.ds(pl.multiple_of(j * 256, 256), 256)
            both = jnp.dot(picked[...], raw[i, :, cols], preferred_element_type=jnp.float32).astype(jnp.bfloat16)
            cand[i, 2 * j] = both[:, :WIDTH]
            cand[i, 2 * j + 1] = both[:, WIDTH:]
            return carry

        lax.fori_loop(0, HEADS // 2, pair, 0)

    loads[0].wait()
    candidate(0)
    loads[1].wait()
    candidate(1)
    greeted()
    core_copy = remote(cand.at[1 - c], core_in, core_s, core_r, other_core)
    core_copy.start()
    sort(0, kbuf, HALO)
    send_far(0)
    core_copy.wait_recv()
    half[...] = cand[c] + core_in[...]

    def z_copy(i, k):
        return remote(half.at[pl.ds(k * OWN, OWN)], z_in.at[member], z_s.at[i], z_r.at[member], owner_of(k))

    @pl.when(owner)
    def _():
        for i, k in enumerate(own_next):
            z_copy(i, k).start()
        z_in[member] = half[pl.ds(own * OWN, OWN)]

    @pl.when(jnp.logical_not(owner))
    def _():
        for k in range(OWNERS):
            z_copy(k, k).start()

    sort(1, vbuf, HALO)
    send_far(1)
    loads[2].wait()
    sort(2, qs, 0)

    ones = jnp.ones((1, WIDTH), jnp.bfloat16)

    def scored(q, k, biases):
        scores = lax.dot_general(q, k, (((1,), (1,)), ((), ())), preferred_element_type=jnp.float32) * SCALE
        if biases is not None:
            scores = jnp.concatenate(
                [scores[:, i * TILE : (i + 1) * TILE] + bias for i, bias in enumerate(biases)], axis=1
            )
        return scores

    def widened(v):
        return jnp.concatenate([v, jnp.broadcast_to(ones, v.shape)], axis=1)

    def bias_of(t, b):
        return jnp.where(lists[t, b - t + BAND] >= 0, 0.0, MASKED).astype(jnp.float32)

    def local(h, carry):
        for t in range(TILES):
            low, high = max(0, t - BAND), min(TILES, t + BAND + 1)
            keys = slice(HALO + low * TILE, HALO + high * TILE)
            here = slice(t * TILE, (t + 1) * TILE)
            scores = scored(qs[h, here], kbuf[h, keys], [bias_of(t, b) for b in range(low, high)])
            top = jnp.broadcast_to(jnp.max(scores, axis=1, keepdims=True), (TILE, WIDTH))
            weights = jnp.exp2(scores - jnp.tile(top, (1, high - low))).astype(jnp.bfloat16)
            got = jnp.dot(weights, widened(vbuf[h, keys]), preferred_element_type=jnp.float32)
            peak[h, here] = top
            acc[h, here] = got[:, :WIDTH]
            mass[h, here] = got[:, WIDTH:]
        return carry

    def update(h, t, k, v, biases):
        here = slice(t * TILE, (t + 1) * TILE)
        scores = scored(qs[h, here], k, biases)
        old = peak[h, here]
        top = jnp.maximum(old, jnp.broadcast_to(jnp.max(scores, axis=1, keepdims=True), (TILE, WIDTH)))
        weights = jnp.exp2(scores - jnp.tile(top, (1, k.shape[0] // TILE))).astype(jnp.bfloat16)
        got = jnp.dot(weights, widened(v), preferred_element_type=jnp.float32)
        keep = jnp.exp2(old - top)
        return top, acc[h, here] * keep + got[:, :WIDTH], mass[h, here] * keep + got[:, WIDTH:]

    lax.fori_loop(0, 2, local, 0)

    def y_copy(d):
        rows = pl.ds(pl.multiple_of((y + d) % NY * YROWS, YROWS), YROWS)
        return remote(zsum.at[:, rows], y_in.at[d - 1], y_s.at[d - 1], y_r.at[d - 1], y_to[d - 1])

    @pl.when(owner)
    def _():
        for m in range(GROUP):
            @pl.when(member != m)
            def _():
                remote(half.at[pl.ds(0, OWN)], z_in.at[m], z_s.at[0], z_r.at[m], in_group(m)).wait_recv()

        zsum[...] = ((z_in[0] + z_in[1]) + (z_in[2] + z_in[3])) + (z_in[4] + z_in[5])
        for d in range(1, NY):
            y_copy(d).start()

    send_near(0)
    send_near(1)
    forward(0)
    lax.fori_loop(2, 4, local, 0)

    zz_copy = remote(ysum, zz_in, zz_s, zz_r, partner)

    @pl.when(owner)
    def _():
        for d in range(1, NY):
            y_copy(d).wait_recv()
        total = zsum[:, pl.ds(pl.multiple_of(y * YROWS, YROWS), YROWS)]
        for d in range(1, NY):
            total = total + y_in[d - 1]
        ysum[...] = total
        zz_copy.start()

    forward(1)
    lax.fori_loop(4, 6, local, 0)

    k_here = lax.rem(own + OWNERS, OWNERS)
    rows_here = gbuf.at[c, x, k_here, y]

    def ya_copy(d):
        return remote(rows_here, rows_here, ya_s.at[d - 1], ya_r.at[d - 1], y_to[d - 1])

    @pl.when(owner)
    def _():
        zz_copy.wait_recv()
        gbuf[c, x, k_here, y] = ysum[...] + zz_in[...]
        for d in range(1, NY):
            ya_copy(d).start()

    lax.fori_loop(6, 8, local, 0)

    def za_copy(m):
        piece = gbuf.at[c, x, k_here]
        return remote(piece, piece, za_s.at[m], za_r.at[k_here], in_group(m))

    @pl.when(owner)
    def _():
        for d in range(1, NY):
            ya_copy(d).wait_recv()
        for m in range(GROUP):
            pl.when(member != m)(lambda: za_copy(m).start())

    def xa_copy(k, d):
        piece = gbuf.at[c, x, k]
        return remote(piece, piece, xa_s.at[k, d - 1], xa_r.at[k, d - 1], x_to[d - 1])

    def ca_copy(k, d):
        piece = gbuf.at[c, (x - d + NX) % NX, k]
        return remote(piece, piece, ca_s.at[k, d], ca_r.at[k, d], other_core)

    for k in range(OWNERS):
        @pl.when(own != k)
        def _():
            piece = gbuf.at[c, x, k]
            remote(piece, piece, za_s.at[0], za_r.at[k], in_group(0)).wait_recv()

        for d in range(1, NX):
            xa_copy(k, d).start()
        ca_copy(k, 0).start()

    def side(way, last):
        def head(h, carry):
            cols = pl.ds(pl.multiple_of(h * WIDTH, WIDTH), WIDTH)
            for t in (0, 1) if way == 0 else (2, 3):
                low, high = (t - BAND, 0) if way == 0 else (TILES, t + BAND + 1)
                keys = slice(HALO + low * TILE, HALO + high * TILE)
                here = slice(t * TILE, (t + 1) * TILE)
                biases = [bias_of(t, b) for b in range(low, high)]
                top, sums, share = update(h, t, kbuf[h, keys], vbuf[h, keys], biases)
                if last:
                    att[here, cols] = (sums / share).astype(jnp.bfloat16)
                else:
                    peak[h, here] = top
                    acc[h, here] = sums
                    mass[h, here] = share
            return carry

        lax.fori_loop(0, HEADS, head, 0)

    def near_side():
        for way in range(2):
            @pl.when((z == 0) == (way == 1))
            def _():
                halo_landed(way, False)
                side(way, not NEAR_FIRST)

    def globals_(h, carry):
        k = gbuf[0, :, h // OWN, :, h % OWN].reshape(NG * TILE, WIDTH)
        v = gbuf[1, :, h // OWN, :, h % OWN].reshape(NG * TILE, WIDTH)
        cols = pl.ds(pl.multiple_of(h * WIDTH, WIDTH), WIDTH)
        for t in range(TILES):
            here = slice(t * TILE, (t + 1) * TILE)
            top, sums, share = update(h, t, k, v, None)
            peak[h, here] = top
            acc[h, here] = sums
            mass[h, here] = share
            if NEAR_FIRST:
                att[here, cols] = (sums / share).astype(jnp.bfloat16)
        return carry

    if NEAR_FIRST:
        near_side()
    for k in range(OWNERS + 1):
        if k < OWNERS:
            for d in range(1, NX):
                xa_copy(k, d).wait_recv()
                ca_copy(k, d).start()
        if k > 0:
            for d in range(NX):
                ca_copy(k - 1, d).wait_recv()
            lax.fori_loop(OWN * (k - 1), OWN * k, globals_, 0)
    if not NEAR_FIRST:
        near_side()

    for way in range(2):
        @pl.when((z == 0) == (way == 0))
        def _():
            halo_landed(way, True)
            halo_landed(way, False)
            side(way, True)

    sub = lax.broadcasted_iota(jnp.int32, (ROWS, ROWS), 0)
    perm[...] = jnp.where(jnp.broadcast_to(row, (ROWS, ROWS)) == sub, 1.0, 0.0).astype(jnp.bfloat16)
    stores = []
    for i in range(HEADS // 2):
        cols = slice(i * 256, (i + 1) * 256)
        outv[:, cols] = jnp.dot(perm[...], att[:, cols], preferred_element_type=jnp.float32).astype(jnp.bfloat16)
        store = pltpu.make_async_copy(outv.at[:, cols], out.at[:, cols], out_sem.at[i])
        store.start()
        stores.append(store)
    halo_sent()

    @pl.when(owner)
    def _():
        for i, k in enumerate(own_next):
            z_copy(i, k).wait_send()
        for d in range(1, NY):
            y_copy(d).wait_send()
            ya_copy(d).wait_send()
        zz_copy.wait_send()
        for m in range(GROUP):
            pl.when(member != m)(lambda: za_copy(m).wait_send())

    @pl.when(jnp.logical_not(owner))
    def _():
        for k in range(OWNERS):
            z_copy(k, k).wait_send()

    core_copy.wait_send()
    for k in range(OWNERS):
        for d in range(1, NX):
            xa_copy(k, d).wait_send()
        for d in range(NX):
            ca_copy(k, d).wait_send()
    for store in stores:
        store.wait()


def body(query_rows, key_rows, value_rows, tile_lists, hilbert_order):
    bf16, f32, dma = jnp.bfloat16, jnp.float32, pltpu.SemaphoreType.DMA
    vmem = pltpu.VMEM
    features = HEADS * WIDTH
    padded = ROWS + 2 * HALO
    scratch = [
        vmem((3, ROWS, features), bf16),
        vmem((ROWS, ROWS), bf16),
        vmem((TILE, ROWS), bf16),
        vmem((HEADS, ROWS, WIDTH), bf16),
        vmem((HEADS, padded, WIDTH), bf16),
        vmem((HEADS, padded, WIDTH), bf16),
        vmem((2, 2, HALO, WIDTH), bf16),
        vmem((2, HEADS, TILE, WIDTH), bf16),
        vmem((HEADS, TILE, WIDTH), bf16),
        vmem((HEADS, TILE, WIDTH), bf16),
        vmem((GROUP, OWN, TILE, WIDTH), bf16),
        vmem((OWN, TILE, WIDTH), bf16),
        vmem((NY - 1, OWN, YROWS, WIDTH), bf16),
        vmem((OWN, YROWS, WIDTH), bf16),
        vmem((OWN, YROWS, WIDTH), bf16),
        vmem((2, NX, OWNERS, NY, OWN, YROWS, WIDTH), bf16),
        vmem((HEADS, ROWS, WIDTH), f32),
        vmem((HEADS, ROWS, WIDTH), f32),
        vmem((HEADS, ROWS, WIDTH), f32),
        vmem((ROWS, features), bf16),
        vmem((ROWS, features), bf16),
        dma((3,)),
        dma((HEADS // 2,)),
        dma((2, 2)),
        dma((2, 2, 1 + len(RELAYS))),
        dma((2, len(RELAYS))),
        dma((2, 2)),
        dma((2, 2)),
        dma,
        dma,
        dma((OWNERS,)),
        dma((GROUP,)),
        dma((NY - 1,)),
        dma((NY - 1,)),
        dma,
        dma,
        dma((NY - 1,)),
        dma((NY - 1,)),
        dma((GROUP,)),
        dma((OWNERS,)),
        dma((OWNERS, NX - 1)),
        dma((OWNERS, NX - 1)),
        dma((OWNERS, NX)),
        dma((OWNERS, NX)),
    ]
    anywhere = pl.BlockSpec(memory_space=pl.ANY)
    return pl.pallas_call(
        kernel,
        out_shape=jax.ShapeDtypeStruct(query_rows.shape, bf16),
        in_specs=[
            pl.BlockSpec(memory_space=pltpu.SMEM),
            pl.BlockSpec(memory_space=pltpu.VMEM),
            anywhere,
            anywhere,
            anywhere,
        ],
        out_specs=anywhere,
        scratch_shapes=scratch,
        compiler_params=pltpu.CompilerParams(
            collective_id=0, has_side_effects=True, vmem_limit_bytes=60 << 20
        ),
        name="attend",
    )(tile_lists, hilbert_order.reshape(1, ROWS), key_rows, value_rows, query_rows)


def solution(mesh):
    in_specs = (
        P(("blk", "grp"), None),
        P(("blk", "grp"), None),
        P(("blk", "grp"), None),
        P(("blk", "grp"), None),
        P(("blk", "grp")),
    )
    out_specs = P(("blk", "grp"), None)
    return jax.shard_map(body, mesh=mesh, in_specs=in_specs, out_specs=out_specs, check_vma=False)
```

```python
import functools

import jax
import jax.numpy as jnp
from jax import lax
from jax.experimental import pallas as pl
from jax.experimental.pallas import tpu as pltpu
from jax.sharding import PartitionSpec as P

HEADS = 8
WIDTH = 128
TILE = 128
BAND = 2
NG = 4
ROWS = 512
TILES = ROWS // TILE
HALO = BAND * TILE
GSTRIDE = 768
LOG2E = 1.4426950408889634
SCALE = WIDTH**-0.5 * LOG2E
MASKED = -1e30
NX, NY, NZ, NC = 4, 8, 12, 2
YROWS = TILE // NY
GROUP, OWNERS = 6, 4
OWN = HEADS // OWNERS
OWNER_PLANES = tuple(range(GROUP - OWNERS, GROUP + OWNERS))
DIRECT = 4
RELAYS = (9, 10, 2, 1)
NEAR_FIRST = False
MESH = pl.DeviceIdType.MESH


def place(x, y, z, c):
    return ((x * 4 + y % 4) * NC + c, (y // 4) * NZ + z)


def kernel(
    lists, order_row, k_in, v_in, q_in, out,
    raw, perm, picked, qs, kbuf, vbuf, relayed, cand, core_in, half, z_in, zsum, y_in, ysum, zz_in, gbuf,
    peak, mass, acc, att, outv,
    in_sem, out_sem, near_s, halo_r, leg_s, leg_r, relay_s, core_s, core_r, z_s, z_r, y_s, y_r, zz_s, zz_r,
    ya_s, ya_r, za_s, za_r, xa_s, xa_r, ca_s, ca_r,
):
    blk, grp = lax.axis_index("blk"), lax.axis_index("grp")
    x, yl, c = blk // 8, blk // 2 % 4, blk % 2
    yh, z = grp // NZ, grp % NZ
    y = yh * 4 + yl
    flat = blk * 24 + grp
    base = jnp.where(z < GROUP, GROUP - OWNERS, GROUP)
    first, member, own = z // GROUP * GROUP, z % GROUP, z - base
    owner = (own >= 0) & (own < OWNERS)

    def along(step):
        other = (flat + step + 768) % 768
        return (other // 24, other % 24)

    def remote(src, dst, send, recv, device):
        return pltpu.make_async_remote_copy(
            src_ref=src, dst_ref=dst, send_sem=send, recv_sem=recv, device_id=device, device_id_type=MESH
        )

    loads = [
        pltpu.make_async_copy(src, raw.at[i], in_sem.at[i]) for i, src in enumerate((k_in, v_in, q_in))
    ]
    for load in loads:
        load.start()

    other_core = place(x, y, z, 1 - c)
    y_to = [place(x, y + d - jnp.where(y + d >= NY, NY, 0), z, c) for d in range(1, NY)]
    x_to = [place((x + d) % NX, y, z, c) for d in range(1, NX)]
    partner = place(x, y, jnp.where(z < GROUP, z + 4, z - 4), c)
    barrier = pltpu.get_barrier_semaphore()

    def in_group(m):
        return place(x, y, first + m, c)

    def owner_of(k):
        return place(x, y, base + k, c)

    def greet(devices):
        for device in devices:
            pl.semaphore_signal(barrier, inc=1, device_id=device, device_id_type=MESH)

    own_next = [(own + d) % OWNERS for d in range(1, OWNERS)]
    idle = jnp.where(z < GROUP, 0, 10)
    owner_greets = [*y_to, partner, *[owner_of(k) for k in own_next], place(x, y, idle, c), place(x, y, idle + 1, c)]
    other_greets = [owner_of(k) for k in range(OWNERS)]
    after_greets = [along(step) for r in RELAYS for step in (1 + r, r - 11)]
    before_greets = [along(step) for r in RELAYS for step in (r - 12, r)]
    common = [along(-1), along(1), other_core, *x_to]
    greet(common)
    pl.when(owner)(lambda: greet(owner_greets))
    pl.when(jnp.logical_not(owner))(lambda: greet(other_greets))
    pl.when(z == NZ - 1)(lambda: greet(after_greets))
    pl.when(z == 0)(lambda: greet(before_greets))
    for r in RELAYS:
        pl.when(z == r)(functools.partial(greet, [along(step) for step in (-r, 11 - r, -r - 1, 12 - r)]))

    def greeted():
        for plane in range(NZ):
            count = len(common)
            count += len(owner_greets) if plane in OWNER_PLANES else len(other_greets)
            count += 2 * len(RELAYS) if plane in (0, NZ - 1) else 0
            count += 4 if plane in RELAYS else 0
            pl.when(z == plane)(functools.partial(pl.semaphore_wait, barrier, count))

    row = lax.rem(order_row[...], ROWS)
    wide = jnp.broadcast_to(row, (TILE, ROWS)).T
    lane = lax.broadcasted_iota(jnp.int32, (ROWS, TILE), 1)
    for b in range(TILES):
        perm[:, b * TILE : (b + 1) * TILE] = jnp.where(wide == lane + b * TILE, 1.0, 0.0).astype(jnp.bfloat16)

    def sort(which, dst, start):
        def pair(i, carry):
            cols = pl.ds(pl.multiple_of(i * 256, 256), 256)
            both = jnp.dot(perm[...], raw[which, :, cols], preferred_element_type=jnp.float32)
            both = both.astype(jnp.bfloat16)
            dst[2 * i, start : start + ROWS, :] = both[:, :WIDTH]
            dst[2 * i + 1, start : start + ROWS, :] = both[:, WIDTH:]
            return carry

        lax.fori_loop(0, HEADS // 2, pair, 0)

    bufs = (kbuf, vbuf)
    send_rows = (pl.ds(ROWS, HALO), pl.ds(HALO, HALO))
    land_rows = (pl.ds(0, HALO), pl.ds(HALO + ROWS, HALO))

    def straight(i, way, heads):
        here = pl.ds(0, heads)
        return remote(
            bufs[i].at[here, send_rows[way]], bufs[i].at[here, land_rows[way]],
            near_s.at[i, way], halo_r.at[i, way, 0], along(1 - 2 * way),
        )

    def to_relay(i, way, p):
        return remote(
            bufs[i].at[DIRECT + p, send_rows[way]], relayed.at[i, way],
            leg_s.at[i, p], leg_r.at[i, way], along(RELAYS[p] + (1, -12)[way]),
        )

    def from_relay(i, way, p):
        return remote(
            relayed.at[i, way], bufs[i].at[DIRECT + p, land_rows[way]],
            relay_s.at[i, way], halo_r.at[i, way, p + 1], along((0, 11)[way] - RELAYS[p]),
        )

    edges = ((NZ - 1, 0), (0, 1))
    seam_in = (0, NZ - 1)

    def send_far(i):
        for plane, way in edges:
            @pl.when(z == plane)
            def _():
                for p in range(len(RELAYS)):
                    to_relay(i, way, p).start()
                straight(i, way, DIRECT).start()

    def send_near(i):
        for plane, way in edges:
            pl.when(z != plane)(lambda: straight(i, way, HEADS).start())

    def forward(i):
        for p, r in enumerate(RELAYS):
            @pl.when(z == r)
            def _():
                for way in (0, 1) if r >= GROUP else (1, 0):
                    to_relay(i, way, p).wait_recv()
                    from_relay(i, way, p).start()

    def halo_sent():
        for i in range(2):
            for plane, way in edges:
                @pl.when(z == plane)
                def _():
                    for p in range(len(RELAYS)):
                        to_relay(i, way, p).wait_send()
                    straight(i, way, DIRECT).wait_send()

                pl.when(z != plane)(lambda: straight(i, way, HEADS).wait_send())
            for p, r in enumerate(RELAYS):
                @pl.when(z == r)
                def _():
                    for way in range(2):
                        from_relay(i, way, p).wait_send()

    def halo_landed(way, far):
        @pl.when((z == seam_in[way]) == far)
        def _():
            for i in range(2):
                if far:
                    straight(i, way, DIRECT).wait_recv()
                    for p in range(len(RELAYS)):
                        from_relay(i, way, p).wait_recv()
                else:
                    straight(i, way, HEADS).wait_recv()

    spot = lax.rem(lists[0, 2 * BAND + 1], GSTRIDE)
    mine = lax.div(spot, TILES) == flat % (GSTRIDE // TILES)
    parts = [jnp.where(mine & (lax.rem(spot, TILES) == t), 1.0, 0.0).astype(jnp.bfloat16) for t in range(TILES)]
    pick = None
    for t in range(TILES):
        term = perm[t * TILE : (t + 1) * TILE, :] * parts[t]
        pick = term if pick is None else pick + term
    picked[...] = pick

    def candidate(i):
        def pair(j, carry):
            cols = pl.ds(pl.multiple_of(j * 256, 256), 256)
            both = jnp.dot(picked[...], raw[i, :, cols], preferred_element_type=jnp.float32).astype(jnp.bfloat16)
            cand[i, 2 * j] = both[:, :WIDTH]
            cand[i, 2 * j + 1] = both[:, WIDTH:]
            return carry

        lax.fori_loop(0, HEADS // 2, pair, 0)

    loads[0].wait()
    candidate(0)
    loads[1].wait()
    candidate(1)
    greeted()
    core_copy = remote(cand.at[1 - c], core_in, core_s, core_r, other_core)
    core_copy.start()
    sort(0, kbuf, HALO)
    core_copy.wait_recv()
    half[...] = cand[c] + core_in[...]

    def z_copy(i, k):
        return remote(half.at[pl.ds(k * OWN, OWN)], z_in.at[member], z_s.at[i], z_r.at[member], owner_of(k))

    @pl.when(owner)
    def _():
        for i, k in enumerate(own_next):
            z_copy(i, k).start()
        z_in[member] = half[pl.ds(own * OWN, OWN)]

    @pl.when(jnp.logical_not(owner))
    def _():
        for k in range(OWNERS):
            z_copy(k, k).start()

    send_far(0)
    sort(1, vbuf, HALO)
    send_far(1)
    loads[2].wait()
    sort(2, qs, 0)

    ones = jnp.ones((1, WIDTH), jnp.bfloat16)

    def scored(q, k, biases):
        scores = lax.dot_general(q, k, (((1,), (1,)), ((), ())), preferred_element_type=jnp.float32) * SCALE
        if biases is not None:
            scores = jnp.concatenate(
                [scores[:, i * TILE : (i + 1) * TILE] + bias for i, bias in enumerate(biases)], axis=1
            )
        return scores

    def widened(v):
        return jnp.concatenate([v, jnp.broadcast_to(ones, v.shape)], axis=1)

    def bias_of(t, b):
        return jnp.where(lists[t, b - t + BAND] >= 0, 0.0, MASKED).astype(jnp.float32)

    def local(h, carry):
        for t in range(TILES):
            low, high = max(0, t - BAND), min(TILES, t + BAND + 1)
            keys = slice(HALO + low * TILE, HALO + high * TILE)
            here = slice(t * TILE, (t + 1) * TILE)
            scores = scored(qs[h, here], kbuf[h, keys], [bias_of(t, b) for b in range(low, high)])
            top = jnp.broadcast_to(jnp.max(scores, axis=1, keepdims=True), (TILE, WIDTH))
            weights = jnp.exp2(scores - jnp.tile(top, (1, high - low))).astype(jnp.bfloat16)
            got = jnp.dot(weights, widened(vbuf[h, keys]), preferred_element_type=jnp.float32)
            peak[h, here] = top
            acc[h, here] = got[:, :WIDTH]
            mass[h, here] = got[:, WIDTH:]
        return carry

    def update(h, t, k, v, biases):
        here = slice(t * TILE, (t + 1) * TILE)
        scores = scored(qs[h, here], k, biases)
        old = peak[h, here]
        top = jnp.maximum(old, jnp.broadcast_to(jnp.max(scores, axis=1, keepdims=True), (TILE, WIDTH)))
        weights = jnp.exp2(scores - jnp.tile(top, (1, k.shape[0] // TILE))).astype(jnp.bfloat16)
        got = jnp.dot(weights, widened(v), preferred_element_type=jnp.float32)
        keep = jnp.exp2(old - top)
        return top, acc[h, here] * keep + got[:, :WIDTH], mass[h, here] * keep + got[:, WIDTH:]

    lax.fori_loop(0, 2, local, 0)

    def y_copy(d):
        rows = pl.ds(pl.multiple_of((y + d) % NY * YROWS, YROWS), YROWS)
        return remote(zsum.at[:, rows], y_in.at[d - 1], y_s.at[d - 1], y_r.at[d - 1], y_to[d - 1])

    @pl.when(owner)
    def _():
        for m in range(GROUP):
            @pl.when(member != m)
            def _():
                remote(half.at[pl.ds(0, OWN)], z_in.at[m], z_s.at[0], z_r.at[m], in_group(m)).wait_recv()

        zsum[...] = ((z_in[0] + z_in[1]) + (z_in[2] + z_in[3])) + (z_in[4] + z_in[5])
        for d in range(1, NY):
            y_copy(d).start()

    send_near(0)
    forward(0)
    lax.fori_loop(2, 4, local, 0)

    zz_copy = remote(ysum, zz_in, zz_s, zz_r, partner)

    @pl.when(owner)
    def _():
        for d in range(1, NY):
            y_copy(d).wait_recv()
        total = zsum[:, pl.ds(pl.multiple_of(y * YROWS, YROWS), YROWS)]
        for d in range(1, NY):
            total = total + y_in[d - 1]
        ysum[...] = total
        zz_copy.start()

    forward(1)
    lax.fori_loop(4, 6, local, 0)

    k_here = lax.rem(own + OWNERS, OWNERS)
    rows_here = gbuf.at[c, x, k_here, y]

    def ya_copy(d):
        return remote(rows_here, rows_here, ya_s.at[d - 1], ya_r.at[d - 1], y_to[d - 1])

    @pl.when(owner)
    def _():
        zz_copy.wait_recv()
        gbuf[c, x, k_here, y] = ysum[...] + zz_in[...]
        for d in range(1, NY):
            ya_copy(d).start()

    lax.fori_loop(6, 8, local, 0)

    def za_copy(m):
        piece = gbuf.at[c, x, k_here]
        return remote(piece, piece, za_s.at[m], za_r.at[k_here], in_group(m))

    @pl.when(owner)
    def _():
        for d in range(1, NY):
            ya_copy(d).wait_recv()
        for m in range(GROUP):
            pl.when(member != m)(lambda: za_copy(m).start())

    send_near(1)

    def xa_copy(k, d):
        piece = gbuf.at[c, x, k]
        return remote(piece, piece, xa_s.at[k, d - 1], xa_r.at[k, d - 1], x_to[d - 1])

    def ca_copy(k, d):
        piece = gbuf.at[c, (x - d + NX) % NX, k]
        return remote(piece, piece, ca_s.at[k, d], ca_r.at[k, d], other_core)

    for k in range(OWNERS):
        @pl.when(own != k)
        def _():
            piece = gbuf.at[c, x, k]
            remote(piece, piece, za_s.at[0], za_r.at[k], in_group(0)).wait_recv()

        for d in range(1, NX):
            xa_copy(k, d).start()
        ca_copy(k, 0).start()

    def side(way, last):
        def head(h, carry):
            cols = pl.ds(pl.multiple_of(h * WIDTH, WIDTH), WIDTH)
            for t in (0, 1) if way == 0 else (2, 3):
                low, high = (t - BAND, 0) if way == 0 else (TILES, t + BAND + 1)
                keys = slice(HALO + low * TILE, HALO + high * TILE)
                here = slice(t * TILE, (t + 1) * TILE)
                biases = [bias_of(t, b) for b in range(low, high)]
                top, sums, share = update(h, t, kbuf[h, keys], vbuf[h, keys], biases)
                if last:
                    att[here, cols] = (sums / share).astype(jnp.bfloat16)
                else:
                    peak[h, here] = top
                    acc[h, here] = sums
                    mass[h, here] = share
            return carry

        lax.fori_loop(0, HEADS, head, 0)

    def near_side():
        for way in range(2):
            @pl.when((z == 0) == (way == 1))
            def _():
                halo_landed(way, False)
                side(way, not NEAR_FIRST)

    def globals_(h, carry):
        k = gbuf[0, :, h // OWN, :, h % OWN].reshape(NG * TILE, WIDTH)
        v = gbuf[1, :, h // OWN, :, h % OWN].reshape(NG * TILE, WIDTH)
        cols = pl.ds(pl.multiple_of(h * WIDTH, WIDTH), WIDTH)
        for t in range(TILES):
            here = slice(t * TILE, (t + 1) * TILE)
            top, sums, share = update(h, t, k, v, None)
            peak[h, here] = top
            acc[h, here] = sums
            mass[h, here] = share
            if NEAR_FIRST:
                att[here, cols] = (sums / share).astype(jnp.bfloat16)
        return carry

    if NEAR_FIRST:
        near_side()
    for k in range(OWNERS + 1):
        if k < OWNERS:
            for d in range(1, NX):
                xa_copy(k, d).wait_recv()
                ca_copy(k, d).start()
        if k > 0:
            for d in range(NX):
                ca_copy(k - 1, d).wait_recv()
            lax.fori_loop(OWN * (k - 1), OWN * k, globals_, 0)
    if not NEAR_FIRST:
        near_side()

    for way in range(2):
        @pl.when((z == 0) == (way == 0))
        def _():
            halo_landed(way, True)
            halo_landed(way, False)
            side(way, True)

    sub = lax.broadcasted_iota(jnp.int32, (ROWS, ROWS), 0)
    perm[...] = jnp.where(jnp.broadcast_to(row, (ROWS, ROWS)) == sub, 1.0, 0.0).astype(jnp.bfloat16)
    stores = []
    for i in range(HEADS // 2):
        cols = slice(i * 256, (i + 1) * 256)
        outv[:, cols] = jnp.dot(perm[...], att[:, cols], preferred_element_type=jnp.float32).astype(jnp.bfloat16)
        store = pltpu.make_async_copy(outv.at[:, cols], out.at[:, cols], out_sem.at[i])
        store.start()
        stores.append(store)
    halo_sent()

    @pl.when(owner)
    def _():
        for i, k in enumerate(own_next):
            z_copy(i, k).wait_send()
        for d in range(1, NY):
            y_copy(d).wait_send()
            ya_copy(d).wait_send()
        zz_copy.wait_send()
        for m in range(GROUP):
            pl.when(member != m)(lambda: za_copy(m).wait_send())

    @pl.when(jnp.logical_not(owner))
    def _():
        for k in range(OWNERS):
            z_copy(k, k).wait_send()

    core_copy.wait_send()
    for k in range(OWNERS):
        for d in range(1, NX):
            xa_copy(k, d).wait_send()
        for d in range(NX):
            ca_copy(k, d).wait_send()
    for store in stores:
        store.wait()


def body(query_rows, key_rows, value_rows, tile_lists, hilbert_order):
    bf16, f32, dma = jnp.bfloat16, jnp.float32, pltpu.SemaphoreType.DMA
    vmem = pltpu.VMEM
    features = HEADS * WIDTH
    padded = ROWS + 2 * HALO
    scratch = [
        vmem((3, ROWS, features), bf16),
        vmem((ROWS, ROWS), bf16),
        vmem((TILE, ROWS), bf16),
        vmem((HEADS, ROWS, WIDTH), bf16),
        vmem((HEADS, padded, WIDTH), bf16),
        vmem((HEADS, padded, WIDTH), bf16),
        vmem((2, 2, HALO, WIDTH), bf16),
        vmem((2, HEADS, TILE, WIDTH), bf16),
        vmem((HEADS, TILE, WIDTH), bf16),
        vmem((HEADS, TILE, WIDTH), bf16),
        vmem((GROUP, OWN, TILE, WIDTH), bf16),
        vmem((OWN, TILE, WIDTH), bf16),
        vmem((NY - 1, OWN, YROWS, WIDTH), bf16),
        vmem((OWN, YROWS, WIDTH), bf16),
        vmem((OWN, YROWS, WIDTH), bf16),
        vmem((2, NX, OWNERS, NY, OWN, YROWS, WIDTH), bf16),
        vmem((HEADS, ROWS, WIDTH), f32),
        vmem((HEADS, ROWS, WIDTH), f32),
        vmem((HEADS, ROWS, WIDTH), f32),
        vmem((ROWS, features), bf16),
        vmem((ROWS, features), bf16),
        dma((3,)),
        dma((HEADS // 2,)),
        dma((2, 2)),
        dma((2, 2, 1 + len(RELAYS))),
        dma((2, len(RELAYS))),
        dma((2, 2)),
        dma((2, 2)),
        dma,
        dma,
        dma((OWNERS,)),
        dma((GROUP,)),
        dma((NY - 1,)),
        dma((NY - 1,)),
        dma,
        dma,
        dma((NY - 1,)),
        dma((NY - 1,)),
        dma((GROUP,)),
        dma((OWNERS,)),
        dma((OWNERS, NX - 1)),
        dma((OWNERS, NX - 1)),
        dma((OWNERS, NX)),
        dma((OWNERS, NX)),
    ]
    anywhere = pl.BlockSpec(memory_space=pl.ANY)
    return pl.pallas_call(
        kernel,
        out_shape=jax.ShapeDtypeStruct(query_rows.shape, bf16),
        in_specs=[
            pl.BlockSpec(memory_space=pltpu.SMEM),
            pl.BlockSpec(memory_space=pltpu.VMEM),
            anywhere,
            anywhere,
            anywhere,
        ],
        out_specs=anywhere,
        scratch_shapes=scratch,
        compiler_params=pltpu.CompilerParams(
            collective_id=0, has_side_effects=True, vmem_limit_bytes=60 << 20
        ),
        name="attend",
    )(tile_lists, hilbert_order.reshape(1, ROWS), key_rows, value_rows, query_rows)


def solution(mesh):
    in_specs = (
        P(("blk", "grp"), None),
        P(("blk", "grp"), None),
        P(("blk", "grp"), None),
        P(("blk", "grp"), None),
        P(("blk", "grp")),
    )
    out_specs = P(("blk", "grp"), None)
    return jax.shard_map(body, mesh=mesh, in_specs=in_specs, out_specs=out_specs, check_vma=False)
```
